32 devices in a mesh: row: 2 (over core), col: 4 (over z), dp: 4 (over y, x).
Axes of the slice: x: 2, y: 2, z: 4, core: 2. Of those that a mesh axis runs over, the one named last changes fastest.
Arguments:
- activations: bfloat16 [4, 256, 16384], P('dp', 'col', 'row'), may hold values from -6 to 6
- out_grads: bfloat16 [4, 256, 4096], P('dp', 'row', 'col'), may hold values from -6 to 6
- block_mask: int32 [128, 32], P('row', 'col'), may hold values from 0 to 1, as said below
- master_weight: float32 [16384, 4096], P(('row', 'dp'), 'col'), may hold values from -0.046875 to 0.046875
- first_moment: float32 [16384, 4096], P(('row', 'dp'), 'col'), may hold values from -12 to 12
- second_moment: float32 [16384, 4096], P(('row', 'dp'), 'col'), may hold values from 0.05 to 2
Outputs:
- input_grads: bfloat16 [4, 256, 16384], P('dp', 'col', 'row')
- new_weight: float32 [16384, 4096], P(('row', 'dp'), 'col')
- new_first: float32 [16384, 4096], P(('row', 'dp'), 'col')
- new_second: float32 [16384, 4096], P(('row', 'dp'), 'col')
The draws below stay inside these ranges and needn't reach their ends.
Inputs may be any that keep to these rules, and one draw needn't show every extreme that they name: `block_mask`: 1 where the 128 x 128 block of the weight is kept, 0 where it is pruned.
All inputs are finite; a program needn't handle non-finite values.
Results may differ from the reference program's by a relative error of at most 0.015.
Values may be sent and summed in bfloat16 or wider, within the bound.
A program may use at most 192 MiB of HBM per device.

```python
import math
import jax
import jax.numpy as jnp
from jax import lax

D = 4096
FF = 16384
BLOCK = 128
TOK_G = 256
GROUPS = 4
N_COL = 4


def draw_block_mask(key, part):
    band_key = jax.random.fold_in(key, 11)
    cell_key = jax.random.fold_in(key, 12)
    levels = jax.random.randint(band_key, (FF // BLOCK // 4, 1), 15, 86)
    levels = jnp.repeat(levels, 4, axis=0)
    scores = jax.random.randint(cell_key, (FF // BLOCK, D // BLOCK), 0, 100)
    return (scores < levels).astype(jnp.int32)


def with_spikes(result, own_key, source, target, shards_of, factor):
    def block_of(position):
        return (jnp.arange(result.shape[position]) // (result.shape[position] // shards_of)).reshape((-1,) + (1,) * (result.ndim - 1 - position))

    first = jax.random.permutation(own_key, shards_of)[block_of(target)]
    second = (block_of(target) + shards_of // 2) % shards_of
    return jnp.where((block_of(source) == first) | (block_of(source) == second), factor * result, result)


def shard_levels(stream_key, shape, pieces, low, top_value):
    factor_of, own = 1.0, jax.random.fold_in(stream_key, 6)
    for position, blocks in pieces:
        steps = jnp.exp(jax.random.uniform(jax.random.fold_in(own, position), (blocks,), jnp.float32, low / len(pieces), top_value / len(pieces)))
        factor_of = factor_of * jnp.repeat(steps, shape[position] // blocks).reshape([-1 if axis == position else 1 for axis in range(len(shape))])
    return factor_of


def bell_draw(key, shape, width, reach, shards=(), held_as=jnp.bfloat16):
    loudness = shard_levels(key, shape, shards, -0.22, 0.18) if shards else 1.0
    drawn = jax.random.normal(key, shape, jnp.float32) * width * loudness
    return jnp.minimum(jnp.maximum(drawn, -reach), reach).astype(held_as)


def gaussian_with(rng, shape, width, bound, cuts, heavy, kind=jnp.bfloat16):
    drawn = width * jax.random.normal(rng, shape, jnp.float32)
    if cuts:
        drawn = drawn * shard_levels(rng, shape, cuts, -0.22, 0.18)
    return jnp.clip(with_spikes(drawn, jax.random.fold_in(rng, 3), *heavy), -bound, bound).astype(kind)


def setup_inputs(seed: int = 0) -> dict:
    seeds = jax.random.split(jax.random.key(seed), 7)
    activations = bell_draw(seeds[0], (GROUPS, TOK_G, FF), 1.0, 6.0, ((0, 4), (1, 4), (2, 2)))
    out_grads = gaussian_with(seeds[1], (GROUPS, TOK_G, D), 1.0, 6.0, ((0, 4), (1, 2), (2, 4)), (2, 1, 4, 2.0))
    block_mask = draw_block_mask(jax.random.fold_in(seeds[6], 71), 0)
    master_weight = bell_draw(seeds[3], (FF, D), FF ** -0.5, 0.046875, ((0, 8), (1, 4)), jnp.float32)
    first_moment = bell_draw(seeds[4], (FF, D), 2.0, 12.0, ((0, 8), (1, 4)), jnp.float32)
    second_moment = jnp.clip(jnp.exp(math.log(2.0) - 3.6888794 * jax.random.uniform(seeds[5], (FF, D), jnp.float32) ** shard_levels(seeds[5], (FF, D), ((0, 8), (1, 4)), -0.2, 0.2)), 0.05, 2.0)
    return dict(activations=activations, out_grads=out_grads, block_mask=block_mask, master_weight=master_weight, first_moment=first_moment, second_moment=second_moment)


first_decay = 0.9
second_decay = 0.999
learn_rate = 0.001
adam_epsilon = 1e-08
first_correct = 1.0 - 0.9 ** 10
second_correct = 1.0 - 0.999 ** 10

def expand(block_keep):
    tall, broad = block_keep.shape
    values = block_keep.astype(jnp.float32)
    grown = jnp.broadcast_to(values[:, None, :, None], (tall, BLOCK, broad, BLOCK))
    return grown.reshape(tall * BLOCK, broad * BLOCK)

def reference(activations, out_grads, block_mask, master_weight, first_moment, second_moment):
    keep = expand(block_mask)
    pruned = master_weight.astype(jnp.bfloat16) * keep.astype(jnp.bfloat16)
    col_width = D // N_COL

    def group_inputs(grad_group):

        def add_column(index, running):
            offset = (index * col_width).astype(jnp.int32)
            grad_cols = lax.dynamic_slice_in_dim(grad_group, offset, col_width, 1)
            weight_cols = lax.dynamic_slice_in_dim(pruned, offset, col_width, 1)
            partial_value = jnp.dot(grad_cols, weight_cols.T, preferred_element_type=jnp.float32)
            rounded = lax.optimization_barrier(partial_value.astype(jnp.bfloat16))
            return running + rounded.astype(jnp.float32)
        start_sum = jnp.zeros((grad_group.shape[0], FF), jnp.float32)
        return lax.fori_loop(jnp.int32(0), jnp.int32(N_COL), add_column, start_sum).astype(jnp.bfloat16)
    input_grads = lax.map(group_inputs, out_grads)

    def add_group(running, operands):
        acts_group, grad_group = operands
        partial_value = jnp.dot(acts_group.T, grad_group, preferred_element_type=jnp.float32) * keep
        rounded = lax.optimization_barrier(partial_value.astype(jnp.bfloat16))
        return (running + rounded.astype(jnp.float32), None)
    grad, _ = lax.scan(add_group, jnp.zeros((FF, D), jnp.float32), (activations, out_grads))
    new_first = first_decay * first_moment + (1.0 - first_decay) * grad
    new_second = second_decay * second_moment + (1.0 - second_decay) * grad * grad
    step_size = new_first / first_correct / (jnp.sqrt(new_second / second_correct) + adam_epsilon)
    new_weight = keep * (master_weight - learn_rate * step_size)
    return (input_grads, new_weight, new_first, new_second)
```

```python
import jax
import jax.numpy as jnp
from jax import lax
from jax.sharding import PartitionSpec as P

BLOCK = 128


first_decay = 0.9
second_decay = 0.999
learn_rate = 0.001
adam_epsilon = 1e-08
first_correct = 1.0 - 0.9**10
second_correct = 1.0 - 0.999**10


def expand(block_keep):
    tall, broad = block_keep.shape
    values = block_keep.astype(jnp.float32)
    grown = jnp.broadcast_to(values[:, None, :, None], (tall, BLOCK, broad, BLOCK))
    return grown.reshape(tall * BLOCK, broad * BLOCK)


def body(activations, out_grads, block_mask, master_weight, first_moment, second_moment):
    groups = lax.axis_size("dp")
    cols = lax.axis_size("col")
    shard_rows, shard_cols = master_weight.shape
    part = activations.shape[1]
    shard_blocks = shard_rows // BLOCK
    group_index = lax.axis_index("dp")
    keep_blocks = lax.dynamic_slice_in_dim(
        block_mask, group_index * shard_blocks, shard_blocks, 0
    )
    keep_shard = expand(keep_blocks)
    cotangents = lax.all_gather(out_grads[0], ("dp", "row"), axis=0, tiled=True)
    cotangents = (
        cotangents.reshape(groups, cols, part, shard_cols)
        .transpose(1, 0, 2, 3)
        .reshape(cols * groups * part, shard_cols)
    )
    acts = lax.all_to_all(activations[0], "dp", split_axis=1, concat_axis=0, tiled=True)
    acts = lax.all_gather(acts, "col", axis=0, tiled=True)
    pruned = master_weight.astype(jnp.bfloat16) * keep_shard.astype(jnp.bfloat16)
    partial = lax.dot_general(
        cotangents, pruned, (((1,), (1,)), ((), ())), preferred_element_type=jnp.float32
    ).astype(jnp.bfloat16)
    summed = lax.psum_scatter(partial, "col", scatter_dimension=0, tiled=True)
    summed = lax.all_to_all(summed, "dp", split_axis=0, concat_axis=1, tiled=True)
    input_grads = summed[None]
    grad_shard = (
        lax.dot_general(
            acts, cotangents, (((0,), (0,)), ((), ())), preferred_element_type=jnp.float32
        )
        * keep_shard
    )
    new_first = first_decay * first_moment + (1.0 - first_decay) * grad_shard
    new_second = second_decay * second_moment + (1.0 - second_decay) * grad_shard * grad_shard
    step_size = new_first / first_correct / (jnp.sqrt(new_second / second_correct) + adam_epsilon)
    new_weight = keep_shard * (master_weight - learn_rate * step_size)
    return (input_grads, new_weight, new_first, new_second)


def solution(mesh):
    return jax.shard_map(
        body,
        mesh=mesh,
        in_specs=(
            P("dp", "col", "row"),
            P("dp", "row", "col"),
            P("row", "col"),
            P(("row", "dp"), "col"),
            P(("row", "dp"), "col"),
            P(("row", "dp"), "col"),
        ),
        out_specs=(
            P("dp", "col", "row"),
            P(("row", "dp"), "col"),
            P(("row", "dp"), "col"),
            P(("row", "dp"), "col"),
        ),
        check_vma=False,
    )
```

```python
import jax
import jax.numpy as jnp
from jax import lax
from jax.sharding import PartitionSpec as P

BLOCK = 128


first_decay = 0.9
second_decay = 0.999
learn_rate = 0.001
adam_epsilon = 1e-08
first_correct = 1.0 - 0.9**10
second_correct = 1.0 - 0.999**10


def expand(block_keep):
    tall, broad = block_keep.shape
    values = block_keep.astype(jnp.float32)
    grown = jnp.broadcast_to(values[:, None, :, None], (tall, BLOCK, broad, BLOCK))
    return grown.reshape(tall * BLOCK, broad * BLOCK)


def exchange_groups(mine, groups, width):
    me = lax.axis_index("dp")
    out = jnp.zeros((groups, mine.shape[0], width), mine.dtype)
    for step in range(groups):
        target = lax.rem(me + step, groups)
        source = lax.rem(me + groups - step, groups)
        block = lax.dynamic_slice_in_dim(mine, target * width, width, 1)
        if step:
            block = lax.ppermute(block, "dp", [(i, (i + step) % groups) for i in range(groups)])
        out = lax.dynamic_update_slice_in_dim(out, block[None], source, 0)
    return out


def gather_line(own, cols):
    me = lax.axis_index("col")
    up, down = [own], [own]
    for _ in range(cols - 1):
        up.append(lax.ppermute(up[-1], "col", [(i, i + 1) for i in range(cols - 1)]))
        down.append(lax.ppermute(down[-1], "col", [(i + 1, i) for i in range(cols - 1)]))
    out = jnp.zeros((cols,) + own.shape, own.dtype)
    out = lax.dynamic_update_slice_in_dim(out, own[None], me, 0)
    for step in range(1, cols):
        source = lax.rem(me + cols - step, cols)
        chunk = jnp.where(me >= step, up[step], down[cols - step])
        out = lax.dynamic_update_slice_in_dim(out, chunk[None], source, 0)
    return out


def body(activations, out_grads, block_mask, master_weight, first_moment, second_moment):
    groups = lax.axis_size("dp")
    cols = lax.axis_size("col")
    shard_rows, shard_cols = master_weight.shape
    part = activations.shape[1]
    shard_blocks = shard_rows // BLOCK
    group_index = lax.axis_index("dp")
    keep_blocks = lax.dynamic_slice_in_dim(
        block_mask, group_index * shard_blocks, shard_blocks, 0
    )
    keep_shard = expand(keep_blocks)
    cotangents = lax.all_gather(out_grads[0], ("dp", "row"), axis=0, tiled=True)
    cotangents = (
        cotangents.reshape(groups, cols, part, shard_cols)
        .transpose(1, 0, 2, 3)
        .reshape(cols * groups * part, shard_cols)
    )
    acts = exchange_groups(activations[0], groups, shard_rows)
    cotangents, acts = lax.optimization_barrier((cotangents, acts))
    acts = gather_line(acts, cols).reshape(cols * groups * part, shard_rows)
    pruned = master_weight.astype(jnp.bfloat16) * keep_shard.astype(jnp.bfloat16)
    partial = lax.dot_general(
        cotangents, pruned, (((1,), (1,)), ((), ())), preferred_element_type=jnp.float32
    ).astype(jnp.bfloat16)
    summed = lax.psum_scatter(partial, "col", scatter_dimension=0, tiled=True)
    grad_shard = (
        lax.dot_general(
            acts, cotangents, (((0,), (0,)), ((), ())), preferred_element_type=jnp.float32
        )
        * keep_shard
    )
    new_first = first_decay * first_moment + (1.0 - first_decay) * grad_shard
    new_second = second_decay * second_moment + (1.0 - second_decay) * grad_shard * grad_shard
    step_size = new_first / first_correct / (jnp.sqrt(new_second / second_correct) + adam_epsilon)
    new_weight = keep_shard * (master_weight - learn_rate * step_size)
    summed, new_weight, new_first, new_second = lax.optimization_barrier(
        (summed, new_weight, new_first, new_second)
    )
    summed = lax.all_to_all(summed, "dp", split_axis=0, concat_axis=1, tiled=True)
    input_grads = summed[None]
    return (input_grads, new_weight, new_first, new_second)


def solution(mesh):
    return jax.shard_map(
        body,
        mesh=mesh,
        in_specs=(
            P("dp", "col", "row"),
            P("dp", "row", "col"),
            P("row", "col"),
            P(("row", "dp"), "col"),
            P(("row", "dp"), "col"),
            P(("row", "dp"), "col"),
        ),
        out_specs=(
            P("dp", "col", "row"),
            P(("row", "dp"), "col"),
            P(("row", "dp"), "col"),
            P(("row", "dp"), "col"),
        ),
        check_vma=False,
    )
```

```python
import jax
import jax.numpy as jnp
from jax import lax
from jax.sharding import PartitionSpec as P

BLOCK = 128


first_decay = 0.9
second_decay = 0.999
learn_rate = 0.001
adam_epsilon = 1e-08
first_correct = 1.0 - 0.9**10
second_correct = 1.0 - 0.999**10


def expand(block_keep):
    tall, broad = block_keep.shape
    values = block_keep.astype(jnp.float32)
    grown = jnp.broadcast_to(values[:, None, :, None], (tall, BLOCK, broad, BLOCK))
    return grown.reshape(tall * BLOCK, broad * BLOCK)


def exchange_groups(mine, groups, width):
    me = lax.axis_index("dp")
    out = jnp.zeros((groups, mine.shape[0], width), mine.dtype)
    for step in range(groups):
        target = lax.rem(me + step, groups)
        source = lax.rem(me + groups - step, groups)
        block = lax.dynamic_slice_in_dim(mine, target * width, width, 1)
        if step:
            block = lax.ppermute(block, "dp", [(i, (i + step) % groups) for i in range(groups)])
        out = lax.dynamic_update_slice_in_dim(out, block[None], source, 0)
    return out


def shifts(size, step):
    return [(i, (i + step) % size) for i in range(size)]


def gather_axis(own, name, size):
    me = lax.axis_index(name)
    out = jnp.zeros((size,) + own.shape, own.dtype)
    for step in range(size):
        block = lax.ppermute(own, name, shifts(size, step)) if step else own
        out = lax.dynamic_update_slice_in_dim(
            out, block[None], lax.rem(me + size - step, size), 0
        )
    return out


def return_groups(summed, groups):
    me = lax.axis_index("dp")
    _, part, width = summed.shape
    out = jnp.zeros((part, groups * width), summed.dtype)
    for step in range(groups):
        target = lax.rem(me + step, groups)
        source = lax.rem(me + groups - step, groups)
        block = lax.dynamic_index_in_dim(summed, target, 0, keepdims=False)
        if step:
            block = lax.ppermute(block, "dp", shifts(groups, step))
        out = lax.dynamic_update_slice_in_dim(out, block, source * width, 1)
    return out


def gather_line(own, cols):
    me = lax.axis_index("col")
    up, down = [own], [own]
    for _ in range(cols - 1):
        up.append(lax.ppermute(up[-1], "col", [(i, i + 1) for i in range(cols - 1)]))
        down.append(lax.ppermute(down[-1], "col", [(i + 1, i) for i in range(cols - 1)]))
    out = jnp.zeros((cols,) + own.shape, own.dtype)
    out = lax.dynamic_update_slice_in_dim(out, own[None], me, 0)
    for step in range(1, cols):
        source = lax.rem(me + cols - step, cols)
        chunk = jnp.where(me >= step, up[step], down[cols - step])
        out = lax.dynamic_update_slice_in_dim(out, chunk[None], source, 0)
    return out


def sum_line(partial, cols):
    me = lax.axis_index("col")
    up, down = None, None

    def add(index, running):
        mine = lax.dynamic_index_in_dim(partial, jnp.clip(index, 0, cols - 1), 0, False)
        if running is None:
            return mine
        both = mine.astype(jnp.float32) + running.astype(jnp.float32)
        return both.astype(partial.dtype)

    for step in range(1, cols):
        far = cols - step
        up = lax.ppermute(add(me + far, up), "col", [(i, i + 1) for i in range(step)])
        down = lax.ppermute(add(me - far, down), "col", [(i, i - 1) for i in range(far, cols)])
    total = lax.dynamic_index_in_dim(partial, me, 0, False).astype(jnp.float32)
    total = total + up.astype(jnp.float32) + down.astype(jnp.float32)
    return total.astype(partial.dtype)


def body(activations, out_grads, block_mask, master_weight, first_moment, second_moment):
    groups = lax.axis_size("dp")
    cols = lax.axis_size("col")
    shard_rows, shard_cols = master_weight.shape
    part = activations.shape[1]
    shard_blocks = shard_rows // BLOCK
    group_index = lax.axis_index("dp")
    keep_blocks = lax.dynamic_slice_in_dim(
        block_mask, group_index * shard_blocks, shard_blocks, 0
    )
    keep_shard = expand(keep_blocks)
    mine = gather_axis(out_grads[0], "dp", groups)
    acts = exchange_groups(activations[0], groups, shard_rows)
    cotangents = gather_axis(mine, "row", lax.axis_size("row"))
    cotangents = (
        cotangents.transpose(1, 0, 2, 3)
        .reshape(groups, cols, part, shard_cols)
        .transpose(1, 0, 2, 3)
        .reshape(cols * groups * part, shard_cols)
    )
    cotangents, acts = lax.optimization_barrier((cotangents, acts))
    acts = gather_line(acts, cols).reshape(cols * groups * part, shard_rows)
    pruned = master_weight.astype(jnp.bfloat16) * keep_shard.astype(jnp.bfloat16)
    partial = lax.dot_general(
        cotangents, pruned, (((1,), (1,)), ((), ())), preferred_element_type=jnp.float32
    ).astype(jnp.bfloat16)
    summed = sum_line(partial.reshape(cols, groups, part, shard_rows), cols)
    input_grads = return_groups(summed, groups)[None]
    grad_shard = (
        lax.dot_general(
            acts, cotangents, (((0,), (0,)), ((), ())), preferred_element_type=jnp.float32
        )
        * keep_shard
    )
    new_first = first_decay * first_moment + (1.0 - first_decay) * grad_shard
    new_second = second_decay * second_moment + (1.0 - second_decay) * grad_shard * grad_shard
    step_size = new_first / first_correct / (jnp.sqrt(new_second / second_correct) + adam_epsilon)
    new_weight = keep_shard * (master_weight - learn_rate * step_size)
    return (input_grads, new_weight, new_first, new_second)


def solution(mesh):
    return jax.shard_map(
        body,
        mesh=mesh,
        in_specs=(
            P("dp", "col", "row"),
            P("dp", "row", "col"),
            P("row", "col"),
            P(("row", "dp"), "col"),
            P(("row", "dp"), "col"),
            P(("row", "dp"), "col"),
        ),
        out_specs=(
            P("dp", "col", "row"),
            P(("row", "dp"), "col"),
            P(("row", "dp"), "col"),
            P(("row", "dp"), "col"),
        ),
        check_vma=False,
    )
```

```python
import jax
import jax.numpy as jnp
from jax import lax
from jax.sharding import PartitionSpec as P


BLOCK = 128


first_decay = 0.9
second_decay = 0.999
learn_rate = 0.001
adam_epsilon = 1e-08
first_correct = 1.0 - 0.9**10
second_correct = 1.0 - 0.999**10


def expand(block_keep):
    tall, broad = block_keep.shape
    values = block_keep.astype(jnp.float32)
    grown = jnp.broadcast_to(values[:, None, :, None], (tall, BLOCK, broad, BLOCK))
    return grown.reshape(tall * BLOCK, broad * BLOCK)


def exchange_groups(mine, groups, width):
    me = lax.axis_index("dp")
    out = jnp.zeros((groups, mine.shape[0], width), mine.dtype)
    for step in range(groups):
        target = lax.rem(me + step, groups)
        source = lax.rem(me + groups - step, groups)
        block = lax.dynamic_slice_in_dim(mine, target * width, width, 1)
        if step:
            block = lax.ppermute(block, "dp", [(i, (i + step) % groups) for i in range(groups)])
        out = lax.dynamic_update_slice_in_dim(out, block[None], source, 0)
    return out


def shifts(size, step):
    return [(i, (i + step) % size) for i in range(size)]


def gather_axis(own, name, size):
    me = lax.axis_index(name)
    out = jnp.zeros((size,) + own.shape, own.dtype)
    for step in range(size):
        block = lax.ppermute(own, name, shifts(size, step)) if step else own
        out = lax.dynamic_update_slice_in_dim(
            out, block[None], lax.rem(me + size - step, size), 0
        )
    return out


def return_groups(summed, groups):
    me = lax.axis_index("dp")
    _, part, width = summed.shape
    out = jnp.zeros((part, groups * width), summed.dtype)
    for step in range(groups):
        target = lax.rem(me + step, groups)
        source = lax.rem(me + groups - step, groups)
        block = lax.dynamic_index_in_dim(summed, target, 0, keepdims=False)
        if step:
            block = lax.ppermute(block, "dp", shifts(groups, step))
        out = lax.dynamic_update_slice_in_dim(out, block, source * width, 1)
    return out


def upward(first, last):
    return [(i, i + 1) for i in range(first, last)]


def downward(first, last):
    return [(i + 1, i) for i in range(first, last)]


def line(own, make_partial, cols):
    me = lax.axis_index("col")
    last = cols - 1
    up, down = [own], [own]
    if last:
        up.append(lax.ppermute(own, "col", upward(0, last)))
        down.append(lax.ppermute(own, "col", downward(0, last)))
    partial = make_partial()
    run_up, run_down = None, None

    def add(index, running):
        mine = lax.dynamic_index_in_dim(partial, jnp.clip(index, 0, last), 0, False)
        if running is None:
            return mine
        both = mine.astype(jnp.float32) + running.astype(jnp.float32)
        return both.astype(partial.dtype)

    for step in range(1, cols):
        far = cols - step
        sends = (add(me + far, run_up), add(me - far, run_down))
        send_up, send_down = lax.optimization_barrier(sends)
        run_up = lax.ppermute(send_up, "col", upward(0, step))
        run_down = lax.ppermute(send_down, "col", downward(far - 1, last))
        if step < last:
            up.append(lax.ppermute(up[-1], "col", upward(step, last)))
            down.append(lax.ppermute(down[-1], "col", downward(0, last - step)))
    total = lax.dynamic_index_in_dim(partial, me, 0, False).astype(jnp.float32)
    if last:
        total = total + run_up.astype(jnp.float32) + run_down.astype(jnp.float32)
    out = jnp.zeros((cols,) + own.shape, own.dtype)
    out = lax.dynamic_update_slice_in_dim(out, own[None], me, 0)
    for step in range(1, cols):
        source = lax.rem(me + cols - step, cols)
        chunk = jnp.where(me >= step, up[step], down[cols - step])
        out = lax.dynamic_update_slice_in_dim(out, chunk[None], source, 0)
    return out, total.astype(partial.dtype)


def step_body(activations, out_grads, block_mask, master_weight, first_moment, second_moment):
    groups = lax.axis_size("dp")
    cols = lax.axis_size("col")
    shard_rows, shard_cols = master_weight.shape
    part = activations.shape[1]
    shard_blocks = shard_rows // BLOCK
    group_index = lax.axis_index("dp")
    keep_blocks = lax.dynamic_slice_in_dim(
        block_mask, group_index * shard_blocks, shard_blocks, 0
    )
    keep_shard = expand(keep_blocks)
    mine = gather_axis(out_grads[0], "dp", groups)
    acts = exchange_groups(activations[0], groups, shard_rows)
    cotangents = gather_axis(mine, "row", lax.axis_size("row"))
    cotangents = (
        cotangents.transpose(1, 0, 2, 3)
        .reshape(groups, cols, part, shard_cols)
        .transpose(1, 0, 2, 3)
        .reshape(cols * groups * part, shard_cols)
    )
    cotangents, _ = lax.optimization_barrier((cotangents, acts))

    def make_partial():
        pruned = master_weight.astype(jnp.bfloat16) * keep_shard.astype(jnp.bfloat16)
        return (
            lax.dot_general(
                cotangents, pruned, (((1,), (1,)), ((), ())), preferred_element_type=jnp.float32
            )
            .astype(jnp.bfloat16)
            .reshape(cols, groups, part, shard_rows)
        )

    acts, summed = line(acts, make_partial, cols)
    acts = acts.reshape(cols * groups * part, shard_rows)
    input_grads = return_groups(summed, groups)[None]
    grad_shard = (
        lax.dot_general(
            acts, cotangents, (((0,), (0,)), ((), ())), preferred_element_type=jnp.float32
        )
        * keep_shard
    )
    new_first = first_decay * first_moment + (1.0 - first_decay) * grad_shard
    new_second = second_decay * second_moment + (1.0 - second_decay) * grad_shard * grad_shard
    step_size = new_first / first_correct / (jnp.sqrt(new_second / second_correct) + adam_epsilon)
    new_weight = keep_shard * (master_weight - learn_rate * step_size)
    return (input_grads, new_weight, new_first, new_second)


def solution(mesh):
    return jax.shard_map(
        step_body,
        mesh=mesh,
        in_specs=(
            P("dp", "col", "row"),
            P("dp", "row", "col"),
            P("row", "col"),
            P(("row", "dp"), "col"),
            P(("row", "dp"), "col"),
            P(("row", "dp"), "col"),
        ),
        out_specs=(
            P("dp", "col", "row"),
            P(("row", "dp"), "col"),
            P(("row", "dp"), "col"),
            P(("row", "dp"), "col"),
        ),
        check_vma=False,
    )
```
